32 devices in a mesh: dp: 4 (over z), param: 8 (over y, x, core).
Axes of the slice: x: 2, y: 2, z: 4, core: 2. Of those that a mesh axis runs over, the one named last changes fastest.
Arguments:
- train_grads: bfloat16 [256, 262144], P('dp', 'param'), may hold values from -6 to 6
- target_grads: bfloat16 [128, 262144], P('dp', 'param'), may hold values from -6 to 6
- projection: bfloat16 [1024, 262144], P('dp', 'param'), may hold values from -0.01171875 to 0.01171875
- first_moment: float32 [8, 4, 8192], P('param', 'dp'), may hold values from -0.3 to 0.3
- second_moment: float32 [8, 4, 8192], P('param', 'dp'), may hold values from 0.001 to 0.1
- owner_map: int32 [8, 4], P('param'), may hold values from 0 to 3, as said below
Outputs:
- similarity: float32 [256, 128], P(('dp', 'param'))
The draws below stay inside these ranges and needn't reach their ends.
Inputs may be any that keep to these rules, and one draw needn't show every extreme that they name: `owner_map`: each row is a permutation of 0 to 3.
All inputs are finite; a program needn't handle non-finite values.
Results may differ from the reference program's by a relative error of at most 0.0029.
Values may be sent and summed in bfloat16 or wider, within the bound.
No kernel may reach another device: no remote copies, remote signals or barrier semaphores. Data moves between devices by JAX's collectives and lax.ppermute only.
A program may use at most 128 MiB of HBM per device.

```python
import math
import jax
import jax.numpy as jnp
from jax import lax

K = 1024
TR_DEV = 64
P_SIZE = 262144
BLK = 8192
TRAIN = 256
TARGETS = 128
N_DP = 4
N_PARAM = 8


def draw_owner_map(key, part):
    row_keys = jax.random.split(jax.random.fold_in(key, 7), N_PARAM)
    return jax.vmap(lambda row_key: jax.random.permutation(row_key, N_DP))(row_keys).astype(jnp.int32)


def block_levels(key, shape, cuts, low, top_value):
    factor_of, own = 1.0, jax.random.fold_in(key, 6)
    for position, shards_of in cuts:
        heights = jnp.exp(jax.random.uniform(jax.random.fold_in(own, position), (shards_of,), jnp.float32, low / len(cuts), top_value / len(cuts)))
        factor_of = factor_of * jnp.repeat(heights, shape[position] // shards_of).reshape([-1 if axis == position else 1 for axis in range(len(shape))])
    return factor_of


def centred(key, extent, deviation, limit, cuts=(), held_as=jnp.bfloat16):
    result = jax.random.normal(key, extent, jnp.float32) * deviation
    if len(cuts) > 0:
        result = block_levels(key, extent, cuts, -0.22, 0.18) * result
    return jnp.clip(result, min=-limit, max=limit).astype(held_as)


def setup_inputs(seed: int = 0) -> dict:
    seeds = jax.random.split(jax.random.key(seed), 7)
    return {
        "train_grads": centred(seeds[0], (TRAIN, P_SIZE), 1.0, 6.0, ((0, 4), (1, 8))),
        "target_grads": centred(seeds[1], (TARGETS, P_SIZE), 1.0, 6.0, ((0, 4), (1, 8))),
        "projection": centred(seeds[2], (K, P_SIZE), P_SIZE ** -0.5, 0.01171875, ((0, 4), (1, 8))),
        "first_moment": centred(seeds[3], (N_PARAM, N_DP, BLK), 0.05, 0.3, ((0, 8), (1, 4)), jnp.float32),
        "second_moment": jnp.clip(jnp.exp(math.log(0.1) - 4.6051702 * jax.random.uniform(seeds[4], (N_PARAM, N_DP, BLK), jnp.float32) ** block_levels(seeds[4], (N_PARAM, N_DP, BLK), ((0, 8), (1, 4)), -0.2, 0.2)), 0.001, 0.1),
        "owner_map": draw_owner_map(jax.random.fold_in(seeds[6], 71), 0),
    }


def precondition(grad_rows, first_full, second_full):
    grad_f32 = grad_rows.astype(jnp.float32)
    upper = 0.9 * first_full + 0.1 * grad_f32
    lower = jnp.sqrt(0.999 * second_full + 0.001 * grad_f32 * grad_f32) + 1e-08
    return (upper / lower).astype(jnp.bfloat16)

def project(grad_rows, projection):
    return lax.dot_general(grad_rows, projection, (((1,), (1,)), ((), ())), preferred_element_type=jnp.float32)

def normalize(features):
    return features * lax.rsqrt(lax.optimization_barrier(jnp.mean(features * features, axis=1, keepdims=True)) + 1e-06)

def reference(train_grads, target_grads, projection, first_moment, second_moment, owner_map):
    group_ids = jnp.arange(N_PARAM).astype(jnp.int32)[:, None]
    owners = owner_map.astype(jnp.int32)
    first_full = first_moment[group_ids, owners].reshape(-1)
    second_full = second_moment[group_ids, owners].reshape(-1)

    def one_block(block_rows):
        return project(precondition(block_rows, first_full, second_full), projection)
    train_features = lax.map(one_block, train_grads.reshape(N_DP, TR_DEV, P_SIZE)).reshape(TRAIN, K)
    target_features = project(target_grads, projection)
    train_unit = normalize(train_features)
    target_unit = normalize(target_features)
    similarity = jnp.dot(train_unit, target_unit.T, precision=lax.Precision.HIGHEST, preferred_element_type=jnp.float32)
    return similarity / math.sqrt(K)
```

```python
import functools
import math

import jax
import jax.numpy as jnp
from jax import lax
from jax.experimental import pallas as pl
from jax.experimental.pallas import tpu as pltpu
from jax.sharding import PartitionSpec as P

UNITS = 32
EDGE_UNITS = 11
TRAIN_CHUNKS = (5, 6, 6, 4)


def precondition(grad_rows, first_full, second_full):
    grad_f32 = grad_rows.astype(jnp.float32)
    upper = 0.9 * first_full + 0.1 * grad_f32
    lower = jnp.sqrt(0.999 * second_full + 0.001 * grad_f32 * grad_f32) + 1e-08
    return (upper / lower).astype(jnp.bfloat16)


def accumulate_kernel(count, rows, edge, has_carry, z_ref, *refs):
    steps = count - 2 if edge else count - 1
    projections = 2 if edge else 1
    refs = list(refs)
    own = refs.pop(0)
    lefts = [refs.pop(0) for _ in range(steps)]
    rights = [refs.pop(0) for _ in range(steps)]
    matrices = [refs.pop(0) for _ in range(projections)]
    carries = [refs.pop(0) for _ in range(projections)] if has_carry else None
    outs = [refs.pop(0) for _ in range(projections)]
    gathered = refs.pop(0)
    place = z_ref[0]

    @pl.when(pl.program_id(0) == 0)
    def _():
        for index, out in enumerate(outs):
            out[...] = carries[index][...] if has_carry else jnp.zeros_like(out)

    def work():
        def put(origin, block):
            gathered[pl.ds(pl.multiple_of(origin * rows, rows), rows), :] = block[...]

        put(place, own)
        for step in range(1, steps + 1):
            pl.when(place >= step)(functools.partial(put, place - step, lefts[step - 1]))
            pl.when(place + step < count)(functools.partial(put, place + step, rights[step - 1]))
        everything = gathered[...]
        for matrix, out in zip(matrices, outs):
            out[...] += lax.dot_general(
                everything, matrix[...], (((1,), (1,)), ((), ())), preferred_element_type=jnp.float32
            )

    if edge:
        pl.when(jnp.logical_and(place > 0, place < count - 1))(work)
    else:
        work()


def accumulate(place, count, own, lefts, rights, projection, start, tile, edge_projection, carries):
    rows, depth = own.shape
    features = projection.shape[0]
    edge = edge_projection is not None
    block = pl.BlockSpec((rows, tile), lambda t, z: (0, t))
    first = start // tile
    matrices = [projection]
    matrix_specs = [pl.BlockSpec((features, tile), lambda t, z: (0, first + t))]
    if edge:
        matrices.append(edge_projection)
        matrix_specs.append(pl.BlockSpec((features, tile), lambda t, z: (0, t)))
    total = pl.BlockSpec((count * rows, features), lambda t, z: (0, 0))
    shape = jax.ShapeDtypeStruct((count * rows, features), jnp.float32)
    carried = list(carries) if carries is not None else []
    bulk = 1 + len(lefts) + len(rights)
    result = pl.pallas_call(
        functools.partial(accumulate_kernel, count, rows, edge, bool(carried)),
        out_shape=[shape] * len(matrices),
        grid_spec=pltpu.PrefetchScalarGridSpec(
            num_scalar_prefetch=1,
            grid=(depth // tile,),
            in_specs=[block] * bulk + matrix_specs + [total] * len(carried),
            out_specs=[total] * len(matrices),
            scratch_shapes=[pltpu.VMEM((count * rows, tile), own.dtype)],
        ),
        compiler_params=pltpu.CompilerParams(
            dimension_semantics=("arbitrary",), vmem_limit_bytes=24 * 1024 * 1024
        ),
        cost_estimate=pl.CostEstimate(
            flops=2 * count * rows * features * depth * len(matrices),
            bytes_accessed=2 * depth * (rows * bulk + features * len(matrices)),
            transcendentals=0,
        ),
    )(place, own, *lefts, *rights, *matrices, *carried)
    return result


def spread(own, count, edge, name):
    steps = count - 2 if edge else count - 1
    lefts, rights = [], []
    right = left = own
    last = count - 1
    for step in range(1, steps + 1):
        onward = [(i, i + 1) for i in range(step - 1, last) if not (edge and i + 1 == last)]
        back = [(i + 1, i) for i in range(0, count - step) if not (edge and i == 0)]
        with jax.named_scope(f"{name}_r{step}"):
            right = lax.ppermute(right, "dp", onward)
        with jax.named_scope(f"{name}_l{step}"):
            left = lax.ppermute(left, "dp", back)
        lefts.append(right)
        rights.append(left)
    return lefts, rights


def exchange(blocks, axes):
    return lax.all_to_all(blocks, axes, split_axis=0, concat_axis=0, tiled=True)


def copies(block, number):
    return jnp.broadcast_to(block[None], (number,) + block.shape)


def per_device(train_grads, target_grads, projection, first_moment, second_moment, owner_map):
    count = lax.axis_size("dp")
    groups = lax.axis_size("param")
    place = lax.axis_index("dp").astype(jnp.int32).reshape(1)
    train_rows, depth = train_grads.shape
    target_rows = target_grads.shape[0]
    features = projection.shape[0]
    unit = depth // UNITS
    border = (UNITS - EDGE_UNITS) * unit

    target_plain = lax.slice_in_dim(target_grads, 0, border, axis=1)
    target_edge = lax.slice_in_dim(target_grads, border, depth, axis=1)
    target_plain_all = spread(target_plain, count, False, "gn")
    target_edge_all = spread(target_edge, count, True, "gf")

    moments = jnp.concatenate((first_moment[0], second_moment[0]), axis=0)
    with jax.named_scope("moments"):
        moments = exchange(copies(moments, count), "dp")
    chosen = jnp.take(moments, owner_map[0], axis=0)
    first_full = chosen[:, 0].reshape(-1)
    second_full = chosen[:, 1].reshape(-1)

    def updates(start, stop):
        return precondition(
            lax.slice_in_dim(train_grads, start, stop, axis=1),
            first_full[start:stop],
            second_full[start:stop],
        )

    train_edge = updates(border, depth)
    train_edge_all = spread(train_edge, count, True, "tf")
    outward = [(0, 1), (count - 1, count - 2)]
    inward = [(1, 0), (count - 2, count - 1)]
    with jax.named_scope("pf"):
        edge_projection = lax.ppermute(
            lax.slice_in_dim(projection, border, depth, axis=1), "dp", outward
        )

    chunks = []
    start = 0
    for index, size in enumerate(TRAIN_CHUNKS):
        stop = start + size * unit
        own = updates(start, stop)
        chunks.append((start, own, spread(own, count, False, f"tn{index}")))
        start = stop

    target_part = accumulate(
        place, count, target_plain, *target_plain_all, projection, 0, unit, None, None
    )
    target_main, target_outer = accumulate(
        place, count, target_edge, *target_edge_all, projection, border, unit, edge_projection, None
    )
    train_main, train_outer = accumulate(
        place, count, train_edge, *train_edge_all, projection, border, unit, edge_projection, None
    )
    with jax.named_scope("gb"):
        target_outer = lax.ppermute(target_outer, "dp", inward)
    with jax.named_scope("tb"):
        train_outer = lax.ppermute(train_outer, "dp", inward)

    target_total = target_part[0] + target_main + target_outer
    target_sums = exchange(target_total.reshape(groups, -1, features), "param").sum(axis=0)
    target_full = exchange(copies(target_sums, count), "dp")
    width = count * features
    energy = jnp.sum(target_full * target_full, axis=(0, 2), keepdims=True) / width
    target_unit = target_full * lax.rsqrt(energy + 1e-06)
    everyone = exchange(copies(target_unit, groups), "param")
    everyone = everyone.transpose(1, 0, 2, 3).reshape(count, -1, features)

    train_total = train_main + train_outer
    for start, own, (lefts, rights) in chunks:
        (train_total,) = accumulate(
            place, count, own, lefts, rights, projection, start, unit, None, (train_total,)
        )
    pieces = exchange(train_total.reshape(count * groups, -1, features), ("dp", "param"))
    train_full = pieces.reshape(count, groups, -1, features).sum(axis=1)
    energy = jnp.sum(train_full * train_full, axis=(0, 2), keepdims=True) / width
    train_unit = train_full * lax.rsqrt(energy + 1e-06)
    rows = train_unit.shape[1]
    similarity = jnp.dot(
        train_unit.transpose(1, 0, 2).reshape(rows, width),
        everyone.transpose(1, 0, 2).reshape(-1, width).T,
        precision=lax.Precision.HIGHEST,
        preferred_element_type=jnp.float32,
    )
    return similarity / math.sqrt(width)


def solution(mesh):
    placed = (
        P("dp", "param"),
        P("dp", "param"),
        P("dp", "param"),
        P("param", "dp", None),
        P("param", "dp", None),
        P("param", None),
    )
    return jax.shard_map(
        per_device, mesh=mesh, in_specs=placed, out_specs=P(("dp", "param"), None), check_vma=False
    )
```
